128 devices in a mesh: ctx: 32 (over z, y, core), head: 4 (over x).
Axes of the slice: x: 4, y: 4, z: 4, core: 2. Of those that a mesh axis runs over, the one named last changes fastest.
Arguments:
- inputs: bfloat16 [32768, 8192], P(('ctx', 'head')), may hold values from -6 to 6
- out_grad: bfloat16 [32768, 8192], P(('ctx', 'head')), may hold values from -0.59765625 to 0.59765625
- input_map: bfloat16 [32768, 1024], P(('ctx', 'head')), may hold values from -0.52734375 to 0.52734375
- output_map: bfloat16 [32768, 1024], P(('ctx', 'head')), may hold values from -0.52734375 to 0.52734375
- log_decay: float32 [32768, 128], P(('ctx', 'head')), may hold values from -1 to 0, as said below
- block_mask: int32 [256, 256], replicated, may hold values from 0 to 1, as said below
Outputs:
- grad_inputs: bfloat16 [32768, 8192], P(('ctx', 'head'))
- grad_input_map: bfloat16 [32768, 1024], P(('ctx', 'head'))
- grad_output_map: bfloat16 [32768, 1024], P(('ctx', 'head'))
- grad_log_decay: float32 [32768, 128], P(('ctx', 'head'))
The draws below stay inside these ranges and needn't reach their ends.
Inputs may be any that keep to these rules, and one draw needn't show every extreme that they name: `log_decay`: every entry is negative. `block_mask`: inside each of the 16 diagonal tiles of 16 rows the mask is 1 on and below the diagonal and 0 above it; every tile below the diagonal tiles is all ones or all zeros; tiles above them are zeros.
All inputs are finite; a program needn't handle non-finite values.
Results may differ from the reference program's by a relative error of at most 0.004.
Values may be sent and summed in bfloat16 or wider, within the bound.
A program may use at most 256 MiB of HBM per device.

```python
import math
from functools import partial
import jax
import jax.numpy as jnp
from jax import lax

HEAD_COUNT = 128
HEAD_DIM = 64
STATE = 128
GROUPS = 8
BLOCK = 256
TOKEN_COUNT = 32768
FEATURES = 8192
GROUP_STATE = 1024


def draw_log_decay(key, part):
    random_subkeys = jax.random.split(key, 7)
    fast_share = 0.5
    slow_low = math.log(0.25 / BLOCK)
    slow_high = math.log(1.0 / BLOCK)
    fast_heads = jax.random.uniform(random_subkeys[0], (HEAD_COUNT,)) < fast_share
    fast_rate = jnp.exp(jax.random.uniform(random_subkeys[1], (HEAD_COUNT,), jnp.float32, math.log(1.0 / 60.0), math.log(1.0 / 20.0)))
    slow_rate = jnp.exp(jax.random.uniform(random_subkeys[2], (HEAD_COUNT,), jnp.float32, slow_low, slow_high))
    per_step = jnp.where(fast_heads, fast_rate, slow_rate)
    block_factor = jnp.exp(jax.random.uniform(random_subkeys[3], (TOKEN_COUNT // BLOCK, 1, HEAD_COUNT), jnp.float32, math.log(0.5), math.log(2.0)))
    block_factor = jnp.broadcast_to(block_factor, (TOKEN_COUNT // BLOCK, BLOCK, HEAD_COUNT)).reshape(TOKEN_COUNT, HEAD_COUNT)
    roughness = jax.random.uniform(random_subkeys[4], (TOKEN_COUNT, HEAD_COUNT), jnp.float32, 0.5, 1.5)
    steady_baseline = -(per_step[None, :] * block_factor * roughness)
    spike_locations = jax.random.randint(random_subkeys[5], (3, HEAD_COUNT), 0, TOKEN_COUNT)
    token_positions = jnp.arange(TOKEN_COUNT)[:, None]
    spike_positions_hit = (token_positions == spike_locations[0][None, :]) | (token_positions == spike_locations[1][None, :]) | (token_positions == spike_locations[2][None, :])
    spike_length = jnp.log(jax.random.uniform(random_subkeys[6], (TOKEN_COUNT, HEAD_COUNT), jnp.float32, 0.55, 0.8))
    return (steady_baseline + jnp.where(spike_positions_hit, spike_length, 0.0)).astype(jnp.float32)


def draw_block_mask(key, part):
    tile_size = BLOCK // 16
    kept_tiles = (jax.random.randint(key, (16, 16), 0, 5) < 3).astype(jnp.int32)
    token_positions = jnp.arange(BLOCK)
    row_tile = token_positions // tile_size
    tile_values = kept_tiles[row_tile[:, None], row_tile[None, :]]
    below = row_tile[:, None] > row_tile[None, :]
    same_tile = row_tile[:, None] == row_tile[None, :]
    lower_inside = same_tile & (token_positions[:, None] >= token_positions[None, :])
    return jnp.where(below, tile_values, jnp.where(lower_inside, 1, 0)).astype(jnp.int32)


def level_of(key, shape, cuts, smallest, high):
    def one(dim, parts):
        steps = jax.random.uniform(jax.random.fold_in(jax.random.fold_in(key, 6), dim), (parts,), jnp.float32, smallest / len(cuts), high / len(cuts))
        return jnp.repeat(jnp.exp(steps), shape[dim] // parts).reshape((-1,) + (1,) * (len(shape) - dim - 1))

    loudness = one(*cuts[0])
    for cut in cuts[1:]:
        loudness = loudness * one(*cut)
    return loudness


def bell_draw(rng, dims, deviation, limit, pieces=(), kind=jnp.bfloat16):
    result = jax.random.normal(rng, dims, jnp.float32) * deviation
    if len(pieces) > 0:
        result = level_of(rng, dims, pieces, -0.22, 0.18) * result
    return jnp.clip(result, min=-limit, max=limit).astype(kind)


def setup_inputs(seed: int = 0) -> dict:
    seeds = jax.random.split(jax.random.key(seed), 7)
    inputs = bell_draw(seeds[0], (TOKEN_COUNT, FEATURES), 1.0, 6.0, ((0, 128),))
    out_grad = bell_draw(seeds[1], (TOKEN_COUNT, FEATURES), 0.1, 0.59765625, ((0, 128),))
    input_map = bell_draw(seeds[2], (TOKEN_COUNT, GROUP_STATE), 0.0884, 0.52734375, ((0, 128),))
    output_map = bell_draw(seeds[3], (TOKEN_COUNT, GROUP_STATE), 0.0884, 0.52734375, ((0, 128),))
    log_decay = draw_log_decay(jax.random.fold_in(seeds[6], 71), 0)
    block_mask = draw_block_mask(jax.random.fold_in(seeds[6], 71), 0)
    return dict(inputs=inputs, out_grad=out_grad, input_map=input_map, output_map=output_map, log_decay=log_decay, block_mask=block_mask)


HIGHEST_PRECISION = lax.Precision.HIGHEST

def product_two(form, first, second):
    return jnp.einsum(form, first, second, precision=HIGHEST_PRECISION)

def block_step(running_state, entries, mask_values):
    block_inputs, block_keys, block_query, block_decay = entries
    per_group = HEAD_COUNT // GROUPS
    levels = jnp.cumsum(block_decay, axis=0)
    query_heads = jnp.repeat(block_query, per_group, axis=1)
    keys_heads = jnp.repeat(block_keys, per_group, axis=1)
    scores = product_two('tgn,sgn->gts', block_query, block_keys)
    scores = jnp.repeat(scores, per_group, axis=0)
    transposed = levels.T
    weight = mask_values[None] * jnp.exp(jnp.minimum(transposed[:, :, None] - transposed[:, None, :], 0.0))
    inside_terms = product_two('hts,shp->thp', weight * scores, block_inputs)
    carried_terms = product_two('thn,hnp->thp', query_heads, running_state) * jnp.exp(levels)[:, :, None]
    closing = jnp.exp(levels[-1:] - levels)
    new_written = product_two('shn,shp->hnp', keys_heads * closing[:, :, None], block_inputs)
    state_next = jnp.exp(levels[-1])[:, None, None] * running_state + new_written
    return (state_next, inside_terms + carried_terms)

def forward(inputs, input_map, output_map, log_decay, mask_values):
    block_count = TOKEN_COUNT // BLOCK
    stacked = (inputs.reshape(block_count, BLOCK, HEAD_COUNT, HEAD_DIM), input_map.reshape(block_count, BLOCK, GROUPS, STATE), output_map.reshape(block_count, BLOCK, GROUPS, STATE), log_decay.reshape(block_count, BLOCK, HEAD_COUNT))
    initial = jnp.zeros((HEAD_COUNT, STATE, HEAD_DIM), jnp.float32)
    stepper = jax.checkpoint(partial(block_step, mask_values=mask_values))
    final_state, outputs = lax.scan(stepper, initial, stacked)
    return outputs.reshape(TOKEN_COUNT, HEAD_COUNT * HEAD_DIM)

def reference(inputs, out_grad, input_map, output_map, log_decay, block_mask):
    mask_values = block_mask.astype(jnp.float32)
    target = out_grad.astype(jnp.float32)

    def objective(first, second, third, fourth):
        return jnp.sum(forward(first, second, third, fourth, mask_values) * target)
    gradients = jax.grad(objective, argnums=(0, 1, 2, 3))(inputs.astype(jnp.float32), input_map.astype(jnp.float32), output_map.astype(jnp.float32), log_decay)
    return (gradients[0].astype(jnp.bfloat16), gradients[1].astype(jnp.bfloat16), gradients[2].astype(jnp.bfloat16), gradients[3])
```

```python
import jax
import jax.numpy as jnp
from jax import lax
from jax.experimental import pallas as pl
from jax.experimental.pallas import tpu as pltpu
from jax.sharding import PartitionSpec as P

HEAD_COUNT = 128
HEAD_DIM = 64
STATE = 128
GROUPS = 8
BLOCK = 256
FEATURES = HEAD_COUNT * HEAD_DIM
SPAN = FEATURES // GROUPS
PER_GROUP = HEAD_COUNT // GROUPS
HALF = BLOCK // 2
DEVICES = 128
PIECE_COLS = 512
AXES = ("ctx", "head")
F32 = jnp.float32
BF16 = jnp.bfloat16


def dot(a, b, ca=1, cb=0):
    return lax.dot_general(a, b, (((ca,), (cb,)), ((), ())), preferred_element_type=F32)


def split_two(a):
    high = a.astype(BF16)
    return high, (a - high.astype(F32)).astype(BF16)


def split_three(a):
    high = a.astype(BF16)
    rest = a - high.astype(F32)
    mid = rest.astype(BF16)
    return high, mid, (rest - mid.astype(F32)).astype(BF16)


def exact_dot(selector, a):
    high, mid, low = split_three(a)
    return (dot(selector, low) + dot(selector, mid)) + dot(selector, high)


def spread(a, chooser):
    high, mid, low = split_three(a)
    return (dot(low, chooser) + dot(mid, chooser)) + dot(high, chooser)


def head_chooser(first_head, cols):
    rows = lax.broadcasted_iota(jnp.int32, (HEAD_COUNT, cols), 0)
    owner = lax.broadcasted_iota(jnp.int32, (HEAD_COUNT, cols), 1) // HEAD_DIM + first_head
    return (rows == owner).astype(F32).astype(BF16)


def triangle(lower):
    rows = lax.broadcasted_iota(jnp.int32, (BLOCK, BLOCK), 0)
    cols = lax.broadcasted_iota(jnp.int32, (BLOCK, BLOCK), 1)
    keep = rows >= cols if lower else rows <= cols
    return keep.astype(F32).astype(BF16)


def summary_kernel(x_ref, dy_ref, b_ref, c_ref, decay_ref, f_ref, r_ref, level_ref):
    g = pl.program_id(0)

    @pl.when(g == 0)
    def _():
        level_ref[...] = exact_dot(triangle(True), decay_ref[...])

    level = spread(level_ref[...], head_chooser(g * PER_GROUP, SPAN))
    closing = jnp.exp(level[BLOCK - 1 :] - level)
    opening = jnp.exp(level)
    for coef, val_ref, map_ref, out_ref in (
        (closing, x_ref, b_ref, f_ref),
        (opening, dy_ref, c_ref, r_ref),
    ):
        high, low = split_two(coef * val_ref[...].astype(F32))
        turned = map_ref[...].T
        state = (dot(turned, low) + dot(turned, high)).astype(BF16)
        for c in range(SPAN // PIECE_COLS):
            for n in range(STATE // 16):
                out_ref[c, n] = state[
                    n * 16 : (n + 1) * 16, c * PIECE_COLS : (c + 1) * PIECE_COLS
                ]


def inside_kernel(
    x_ref, dy_ref, b_ref, c_ref, level_ref, mask_ref, gx_ref, gb_ref, gc_ref, gl_ref, y_ref
):
    g = pl.program_id(0)
    chooser = head_chooser(g * PER_GROUP, SPAN)
    level = spread(level_ref[...], chooser)
    for i, (t, s) in enumerate(((0, 0), (1, 1), (1, 0))):
        ts = pl.ds(t * HALF, HALF)
        ss = pl.ds(s * HALF, HALF)
        at = t * HALF + HALF // 2 if t == s else HALF - 1
        ref_level = level[at : at + 1]
        a = jnp.exp(level[t * HALF : (t + 1) * HALF] - ref_level)
        b = jnp.exp(ref_level - level[s * HALF : (s + 1) * HALF])
        u = (a * dy_ref[ts, :].astype(F32)).astype(BF16)
        v = (b * x_ref[ss, :].astype(F32)).astype(BF16)
        keep = mask_ref[ts, ss] == 1
        bs = b_ref[ss, :]
        ct = c_ref[ts, :]
        scores = jnp.where(keep, dot(ct, bs, 1, 1), 0.0)
        together = jnp.where(keep, dot(u, v, 1, 1), 0.0)
        score_n = scores.astype(BF16)
        score_t = scores.T.astype(BF16)
        high, low = split_two(together)
        high_t, low_t = split_two(together.T)
        gc = dot(low, bs) + dot(high, bs)
        gb = dot(low_t, ct) + dot(high_t, ct)
        y = a * dot(score_n, v)
        gx = b * dot(score_t, u)
        if i < 2:
            gc_ref[ts, :] = gc
            gb_ref[ss, :] = gb
            y_ref[ts, :] = y
            gx_ref[ss, :] = gx
        else:
            gc_ref[ts, :] += gc
            gb_ref[ss, :] += gb
            y_ref[ts, :] += y
            gx_ref[ss, :] += gx
    term = dy_ref[...].astype(F32) * y_ref[...] - x_ref[...].astype(F32) * gx_ref[...]
    high, low = split_two(term)
    total = dot(low, chooser, 1, 1) + dot(high, chooser, 1, 1)

    @pl.when(g == 0)
    def _():
        gl_ref[...] = total

    @pl.when(g > 0)
    def _():
        gl_ref[...] += total


def scan_kernel(f_ref, r_ref, decay_ref, s_ref, g_ref, wide_ref):
    owner = lax.axis_index("ctx") * 4 + lax.axis_index("head")
    first = (owner // 8) * (PIECE_COLS // HEAD_DIM)
    wide_ref[...] = jnp.exp(spread(decay_ref[...], head_chooser(first, PIECE_COLS)))

    def step(i, carry):
        front, back = carry
        j = DEVICES - 1 - i
        s_ref[i] = front.astype(BF16)
        g_ref[j] = back.astype(BF16)
        front = wide_ref[pl.ds(i, 1), :] * front + f_ref[i].astype(F32)
        back = wide_ref[pl.ds(j, 1), :] * back + r_ref[j].astype(F32)
        return front, back

    zero = jnp.zeros((16, PIECE_COLS), F32)
    lax.fori_loop(0, DEVICES, step, (zero, zero), unroll=8)


def finish_kernel(
    x_ref, dy_ref, b_ref, c_ref, level_ref, s_ref, g_ref, gx_in, gb_in, gc_in, gl_in,
    gx_ref, gb_ref, gc_ref, gd_ref, gl_ref,
):
    g = pl.program_id(0)
    chooser = head_chooser(g * PER_GROUP, SPAN)
    level = spread(level_ref[...], chooser)
    closing = jnp.exp(level[BLOCK - 1 :] - level)
    opening = jnp.exp(level)

    def whole(ref):
        return jnp.concatenate(
            [
                jnp.concatenate([ref[c, n] for n in range(STATE // 16)], axis=0)
                for c in range(SPAN // PIECE_COLS)
            ],
            axis=1,
        )

    state = whole(s_ref)
    leave = whole(g_ref)
    od = opening * dy_ref[...].astype(F32)
    gc_ref[...] = (gc_in[...] + dot(od.astype(BF16), state, 1, 1)).astype(BF16)
    row = od * dot(c_ref[...], state)
    cx = closing * x_ref[...].astype(F32)
    gb_ref[...] = (gb_in[...] + dot(cx.astype(BF16), leave, 1, 1)).astype(BF16)
    back = dot(b_ref[...], leave)
    gx_ref[...] = (gx_in[...] + closing * back).astype(BF16)
    col = cx * back
    last = jnp.sum(col, axis=0, keepdims=True) + jnp.exp(level[BLOCK - 1 :]) * jnp.sum(
        state.astype(F32) * leave.astype(F32), axis=0, keepdims=True
    )
    is_last = lax.broadcasted_iota(jnp.int32, (BLOCK, SPAN), 0) == BLOCK - 1
    high, low = split_two((row - col) + jnp.where(is_last, last, 0.0))
    total = dot(low, chooser, 1, 1) + dot(high, chooser, 1, 1)

    @pl.when(g == 0)
    def _():
        gl_ref[...] = gl_in[...] + total

    @pl.when(g > 0)
    def _():
        gl_ref[...] += total

    @pl.when(g == GROUPS - 1)
    def _():
        gd_ref[...] = exact_dot(triangle(False), gl_ref[...])


def per_device(inputs, out_grad, input_map, output_map, log_decay, block_mask):
    wide = pl.BlockSpec((BLOCK, SPAN), lambda g: (0, g))
    thin = pl.BlockSpec((BLOCK, STATE), lambda g: (0, g))
    heads = pl.BlockSpec((BLOCK, HEAD_COUNT), lambda g: (0, 0))
    square = pl.BlockSpec((BLOCK, BLOCK), lambda g: (0, 0))
    pieces = pl.BlockSpec((SPAN // PIECE_COLS, STATE // 16, 16, PIECE_COLS), lambda g: (g, 0, 0, 0))
    piece_shape = (FEATURES // PIECE_COLS, STATE // 16, 16, PIECE_COLS)
    params = pltpu.CompilerParams(vmem_limit_bytes=56 * 1024 * 1024)
    f, r, level = pl.pallas_call(
        summary_kernel,
        grid=(GROUPS,),
        in_specs=[wide, wide, thin, thin, heads],
        out_specs=[pieces, pieces, heads],
        out_shape=[
            jax.ShapeDtypeStruct(piece_shape, BF16),
            jax.ShapeDtypeStruct(piece_shape, BF16),
            jax.ShapeDtypeStruct((BLOCK, HEAD_COUNT), F32),
        ],
        compiler_params=params,
    )(inputs, out_grad, input_map, output_map, log_decay)
    ends = lax.all_to_all(
        jnp.broadcast_to(level[BLOCK - 1 :], (DEVICES, HEAD_COUNT)), AXES, 0, 0, tiled=True
    )
    flat = (DEVICES, 16, PIECE_COLS)
    sent = jnp.concatenate([f.reshape(flat), r.reshape(flat)], axis=1)
    came = lax.all_to_all(sent, AXES, 0, 0, tiled=True)
    came_f, came_r = came[:, :16], came[:, 16:]
    gx_in, gb_in, gc_in, gl_in = pl.pallas_call(
        inside_kernel,
        grid=(GROUPS,),
        in_specs=[wide, wide, thin, thin, heads, square],
        out_specs=[wide, thin, thin, heads],
        out_shape=[
            jax.ShapeDtypeStruct((BLOCK, FEATURES), F32),
            jax.ShapeDtypeStruct((BLOCK, GROUPS * STATE), F32),
            jax.ShapeDtypeStruct((BLOCK, GROUPS * STATE), F32),
            jax.ShapeDtypeStruct((BLOCK, HEAD_COUNT), F32),
        ],
        scratch_shapes=[pltpu.VMEM((BLOCK, SPAN), F32)],
        compiler_params=params,
    )(inputs, out_grad, input_map, output_map, level, block_mask)
    s, g = pl.pallas_call(
        scan_kernel,
        out_shape=[jax.ShapeDtypeStruct(flat, BF16), jax.ShapeDtypeStruct(flat, BF16)],
        scratch_shapes=[pltpu.VMEM((DEVICES, PIECE_COLS), F32)],
        compiler_params=params,
    )(came_f, came_r, ends)
    back = lax.all_to_all(jnp.concatenate([s, g], axis=1), AXES, 0, 0, tiled=True)
    s, g = back[:, :16].reshape(piece_shape), back[:, 16:].reshape(piece_shape)
    return pl.pallas_call(
        finish_kernel,
        grid=(GROUPS,),
        in_specs=[wide, wide, thin, thin, heads, pieces, pieces, wide, thin, thin, heads],
        out_specs=[wide, thin, thin, heads],
        out_shape=[
            jax.ShapeDtypeStruct((BLOCK, FEATURES), BF16),
            jax.ShapeDtypeStruct((BLOCK, GROUPS * STATE), BF16),
            jax.ShapeDtypeStruct((BLOCK, GROUPS * STATE), BF16),
            jax.ShapeDtypeStruct((BLOCK, HEAD_COUNT), F32),
        ],
        scratch_shapes=[pltpu.VMEM((BLOCK, HEAD_COUNT), F32)],
        compiler_params=params,
    )(inputs, out_grad, input_map, output_map, level, s, g, gx_in, gb_in, gc_in, gl_in)


def solution(mesh):
    split = P(AXES, None)
    return tuple_map(mesh, split)


def tuple_map(mesh, split):
    return jax.shard_map(
        per_device,
        mesh=mesh,
        in_specs=(split, split, split, split, split, P()),
        out_specs=(split, split, split, split),
        check_vma=False,
    )
```
